32 devices in a mesh: blk: 8 (over y, x, core), rows: 4 (over z).
Axes of the slice: x: 2, y: 2, z: 4, core: 2. Of those that a mesh axis runs over, the one named last changes fastest.
Arguments:
- covariance: float32 [16384, 8, 8, 256], P('rows', None, 'blk'), may hold values from 0 to 5, as said below
- panel_order: int32 [64], replicated, may hold values from 0 to 63, each once
Outputs:
- factored: float32 [16384, 8, 8, 256], P('rows', None, 'blk')
The draws below stay inside these ranges and needn't reach their ends.
Inputs may be any that keep to these rules, and one draw needn't show every extreme that they name: covariance is symmetric and positive definite. `panel_order`: every panel appears once; panel j is held by index j % 8 of blk.
All inputs are finite; a program needn't handle non-finite values.
Results may differ from the reference program's by a relative error of at most 0.0003.
Values sent between devices are 32-bit elements; how exact they have to be, the bound alone decides.
A program may use at most 192 MiB of HBM per device.

```python
import jax
import jax.numpy as jnp
from jax import lax

ORDER = 16384
PANEL = 256
SECTIONS = 2
PANELS = 64
OWNERS = 8
PAN_DEV = 8


def draw_covariance(key, part):
    base_key = jax.random.fold_in(key, 11)
    point_key = jax.random.fold_in(base_key, 0)
    points = jax.random.uniform(point_key, (ORDER, 3), jnp.float32)
    squared = jnp.zeros((ORDER, ORDER), jnp.float32)
    for axis_index in range(3):
        column = points[:, axis_index]
        spread_gap = column[:, None] - column[None, :]
        squared = squared + spread_gap * spread_gap
    distance = jnp.sqrt(squared)
    kernel = jnp.exp(-distance / 0.2)
    indices = jnp.arange(ORDER)
    kernel = jnp.where(indices[:, None] == indices[None, :], kernel + 0.25, kernel)
    return kernel.reshape(ORDER, PAN_DEV, OWNERS, PANEL)


def setup_inputs(seed: int = 0) -> dict:
    seeds = jax.random.split(jax.random.key(seed), 3)
    covariance = draw_covariance(jax.random.fold_in(seeds[2], 71), 0)
    panel_order = jax.random.permutation(seeds[1], PANELS).astype(jnp.int32)
    return dict(covariance=covariance, panel_order=panel_order)


def inverse_factor(diagonal_block):
    lower_factor = jnp.linalg.cholesky(diagonal_block)
    identity_block = jnp.eye(diagonal_block.shape[0], dtype=diagonal_block.dtype)
    return lax.linalg.triangular_solve(lower_factor, identity_block, left_side=True, lower=True)

def reference(covariance, panel_order):
    matrix_order = covariance.shape[0]
    panel_width = covariance.shape[3]
    panel_total = matrix_order // panel_width
    working = covariance.reshape(matrix_order, matrix_order)
    frozen = jnp.zeros((panel_total,), jnp.float32)
    for round_index in range(SECTIONS):
        target = panel_order[round_index]
        first_column = (target * panel_width).astype(jnp.int32)
        column_panel = lax.dynamic_slice_in_dim(working, first_column, panel_width, 1)
        diagonal_block = lax.dynamic_slice_in_dim(column_panel, first_column, panel_width, 0)
        inverse = inverse_factor(diagonal_block)
        factor = jnp.dot(column_panel.astype(jnp.float32), inverse.T.astype(jnp.float32), precision=lax.Precision.HIGHEST, preferred_element_type=jnp.float32)
        frozen = frozen + (jnp.arange(panel_total) == target).astype(jnp.float32)
        live_rows = jnp.repeat(1.0 - frozen, panel_width)
        masked_factor = factor * live_rows[:, None]
        working = working - jnp.dot(factor.astype(jnp.float32), masked_factor.T.astype(jnp.float32), precision=lax.Precision.HIGHEST, preferred_element_type=jnp.float32)
        working = lax.dynamic_update_slice_in_dim(working, factor, first_column, 1)
    return working.reshape(covariance.shape)
```

```python
import jax
import jax.numpy as jnp
from jax import lax
from jax.experimental import pallas as pl
from jax.experimental.pallas import tpu as pltpu
from jax.sharding import PartitionSpec as P

SECTIONS = 2
LANES = 128
HIGHEST = lax.Precision.HIGHEST


def split(values):
    high = values.astype(jnp.bfloat16)
    low = (values - high.astype(jnp.float32)).astype(jnp.bfloat16)
    return high, low


def update_kernel(keep_ref, old_ref, left_ref, right_ref, out_ref, right_parts):
    slots, depth, width = right_ref.shape
    rows = left_ref.shape[0]
    chunks = old_ref.shape[0] // rows
    halves = width // LANES

    @pl.when(pl.program_id(0) == 0)
    def _():
        for slot in range(slots):
            high, low = split(right_ref[slot])
            right_parts[slot, :depth, :] = high
            right_parts[slot, depth : 2 * depth, :] = low
            right_parts[slot, 2 * depth :, :] = high

    high, low = split(left_ref[...])
    left_parts = jnp.concatenate([high, high, low], axis=1)
    for slot in range(slots):
        change = jnp.dot(left_parts, right_parts[slot], preferred_element_type=jnp.float32)
        keep = keep_ref[slot] > 0
        for half in range(halves):
            at = pl.ds(slot * halves + half, rows, stride=chunks)
            out_ref[at, :] = jnp.where(keep, old_ref[at, :], 0.0) - change[:, half * LANES : (half + 1) * LANES]


def update(flat, keep, left, right):
    panels, rows, depth = left.shape
    slots, _, width = right.shape
    lines = flat.shape[0] // panels
    return pl.pallas_call(
        update_kernel,
        out_shape=jax.ShapeDtypeStruct(flat.shape, jnp.float32),
        grid_spec=pltpu.PrefetchScalarGridSpec(
            num_scalar_prefetch=1,
            grid=(panels,),
            in_specs=[
                pl.BlockSpec((lines, LANES), lambda i, keep: (i, 0)),
                pl.BlockSpec((None, rows, depth), lambda i, keep: (i, 0, 0)),
                pl.BlockSpec((slots, depth, width), lambda i, keep: (0, 0, 0)),
            ],
            out_specs=pl.BlockSpec((lines, LANES), lambda i, keep: (i, 0)),
            scratch_shapes=[pltpu.VMEM((slots, 3 * depth, width), jnp.bfloat16)],
        ),
        compiler_params=pltpu.CompilerParams(vmem_limit_bytes=56 << 20),
    )(keep, flat, left, right)


def local(covariance, panel_order):
    row_count, slots, _, width = covariance.shape
    owners = lax.axis_size("blk")
    row_blocks = lax.axis_size("rows")
    column_index = lax.axis_index("blk")
    row_index = lax.axis_index("rows")
    targets = [panel_order[section] for section in range(SECTIONS)]
    depth = SECTIONS * width
    row_panels = row_count // width
    view = covariance.reshape(row_count, slots, width)

    own = jnp.concatenate(
        [
            jnp.where(
                target % owners == column_index,
                lax.dynamic_index_in_dim(view, target // owners, 1, keepdims=False),
                0.0,
            )
            for target in targets
        ],
        axis=1,
    )
    block = jnp.concatenate(
        [
            jnp.where(
                target // row_panels == row_index,
                lax.dynamic_slice_in_dim(own, (target % row_panels) * width, width, 0),
                0.0,
            )
            for target in targets
        ],
        axis=0,
    )
    block = lax.psum(block, ("blk", "rows"))

    left = lax.psum(own, "blk").reshape(row_panels, width, depth)
    if row_panels % owners == 0:
        groups = row_panels // owners
        pieces = left.reshape(groups, owners, width, depth)
        mine = lax.dynamic_index_in_dim(pieces, column_index, 1, keepdims=False)
        across = lax.all_gather(mine, "rows", axis=0, tiled=True)
    else:
        across = jnp.concatenate(
            [
                jnp.where(
                    target // row_panels == row_index,
                    lax.dynamic_slice_in_dim(view, (target % row_panels) * width, width, 0),
                    0.0,
                )
                for target in targets
            ],
            axis=0,
        )
        across = lax.psum(across, "rows").transpose(1, 2, 0)

    lower = jnp.linalg.cholesky(block)
    inverse = lax.linalg.triangular_solve(
        lower, jnp.eye(depth, dtype=jnp.float32), left_side=True, lower=True
    )
    whole = jnp.dot(inverse.T, inverse, precision=HIGHEST)
    right = jnp.einsum("dk,pck->pdc", whole, across, precision=HIGHEST)
    slot_panels = jnp.arange(slots, dtype=jnp.int32) * owners + column_index
    keep = jnp.ones((slots,), jnp.int32)
    for section, target in enumerate(targets):
        here = slot_panels == target
        keep = jnp.where(here, 0, keep)
        solved = -inverse[section * width : (section + 1) * width].T
        right = jnp.where(here[:, None, None], solved[None], right)
    flat = covariance.reshape(row_count * slots * (width // LANES), LANES)
    return update(flat, keep, left, right).reshape(covariance.shape)


def solution(mesh):
    return jax.shard_map(
        local,
        mesh=mesh,
        in_specs=(P("rows", None, "blk", None), P()),
        out_specs=P("rows", None, "blk", None),
        check_vma=False,
    )
```

```python
import functools

import jax
import jax.numpy as jnp
from jax import lax
from jax.experimental import pallas as pl
from jax.experimental.pallas import tpu as pltpu
from jax.sharding import PartitionSpec as P

SECTIONS = 2
LANES = 128
CHUNKS = 8
TILE = 128
MESH = pl.DeviceIdType.MESH
HIGHEST = lax.Precision.HIGHEST


def split(values):
    high = values.astype(jnp.bfloat16)
    low = (values - high.astype(jnp.float32)).astype(jnp.bfloat16)
    return high, low


def exchange_kernel(
    row_blocks, owners, chunks, root_ref, side_ref, own_ref, across_ref, left_ref,
    from_low, from_high, to_high, to_low, send_high, send_low, recv_low, recv_high,
    send_chip, recv_chip, send_pair, recv_pair,
):
    z = lax.axis_index("rows")
    me = lax.axis_index("blk")
    last = row_blocks - 1
    chips = owners // 2
    chip, core = me // 2, me % 2
    pair = chip * 2 + 1 - core
    rows = own_ref.shape[0] // chunks
    span = left_ref.shape[2]
    columns = pl.ds(pl.multiple_of(z * span, LANES), span)
    reach = jnp.maximum(z, last - z)

    def lines(c):
        return pl.ds(pl.multiple_of(c * rows, 8), rows)

    def mate(d):
        return (chip + d) % chips * 2 + core

    def source(d):
        return (chip + chips - d) % chips * 2 + core

    def along(src, dst, send, recv, c, step):
        return pltpu.make_async_remote_copy(
            src_ref=src.at[lines(c)], dst_ref=dst.at[lines(c)], send_sem=send.at[c], recv_sem=recv.at[c],
            device_id={"rows": z + step}, device_id_type=MESH,
        )

    def to_mate(d, c):
        return pltpu.make_async_remote_copy(
            src_ref=across_ref.at[lines(c), columns], dst_ref=left_ref.at[me, lines(c)],
            send_sem=send_chip.at[d - 1, c], recv_sem=recv_chip.at[d - 1, c],
            device_id={"blk": mate(d)}, device_id_type=MESH,
        )

    def to_pair(d, c):
        who = source(d)
        src = across_ref.at[lines(c), columns] if d == 0 else left_ref.at[who, lines(c)]
        return pltpu.make_async_remote_copy(
            src_ref=src, dst_ref=left_ref.at[who, lines(c)],
            send_sem=send_pair.at[d, c], recv_sem=recv_pair.at[d, c],
            device_id={"blk": pair}, device_id_type=MESH,
        )

    barrier = pltpu.get_barrier_semaphore()
    for d in range(1, chips):
        pl.semaphore_signal(barrier, inc=1, device_id={"blk": mate(d)}, device_id_type=MESH)
    pl.semaphore_signal(barrier, inc=1, device_id={"blk": pair}, device_id_type=MESH)

    @pl.when(z > 0)
    def _():
        pl.semaphore_signal(barrier, inc=1, device_id={"rows": z - 1}, device_id_type=MESH)

    @pl.when(z < last)
    def _():
        pl.semaphore_signal(barrier, inc=1, device_id={"rows": z + 1}, device_id_type=MESH)

    ends = jnp.where(z > 0, 1, 0) + jnp.where(z < last, 1, 0)
    pl.semaphore_wait(barrier, chips + ends)

    def valid(c):
        return jnp.logical_and(c >= 0, c < chunks)

    def step(t, carry):
        c = t - z

        @pl.when(valid(c))
        def _():
            @pl.when(z == 0)
            def _():
                along(own_ref, from_low, send_high, recv_low, c, 1).start()

            @pl.when(z > 0)
            def _():
                along(to_high, from_low, send_high, recv_low, c, 0).wait_recv()

            @pl.when(jnp.logical_and(z > 0, z < last))
            def _():
                here = root_ref[c] > 0
                to_high[lines(c), :] = jnp.where(here, own_ref[lines(c), :], from_low[lines(c), :])
                along(to_high, from_low, send_high, recv_low, c, 1).start()

        e = t - (last - z)

        @pl.when(valid(e))
        def _():
            @pl.when(z == last)
            def _():
                along(own_ref, from_high, send_low, recv_high, e, -1).start()

            @pl.when(z < last)
            def _():
                along(to_low, from_high, send_low, recv_high, e, 0).wait_recv()

            @pl.when(jnp.logical_and(z > 0, z < last))
            def _():
                here = root_ref[e] > 0
                to_low[lines(e), :] = jnp.where(here, own_ref[lines(e), :], from_high[lines(e), :])
                along(to_low, from_high, send_low, recv_high, e, -1).start()

        f = t - reach

        @pl.when(valid(f))
        def _():
            here = root_ref[f] > 0
            above = side_ref[f] > 0

            @pl.when(z == 0)
            def _():
                across_ref[lines(f), :] = jnp.where(here, own_ref[lines(f), :], from_high[lines(f), :])

            @pl.when(z == last)
            def _():
                across_ref[lines(f), :] = jnp.where(here, own_ref[lines(f), :], from_low[lines(f), :])

            @pl.when(jnp.logical_and(z > 0, z < last))
            def _():
                far = jnp.where(above, from_low[lines(f), :], from_high[lines(f), :])
                across_ref[lines(f), :] = jnp.where(here, own_ref[lines(f), :], far)

            left_ref[me, lines(f), :] = across_ref[lines(f), columns]
            for d in range(1, chips):
                to_mate(d, f).start()
            to_pair(0, f).start()

        g = f - 1

        @pl.when(valid(g))
        def _():
            for d in range(1, chips):
                to_mate(d, g).wait_recv()
                to_pair(d, g).start()

        return carry

    lax.fori_loop(0, chunks + last + 1, step, 0)

    def finish(c, carry):
        @pl.when(z < last)
        def _():
            along(own_ref, from_low, send_high, recv_low, c, 1).wait_send()

        @pl.when(z > 0)
        def _():
            along(own_ref, from_high, send_low, recv_high, c, -1).wait_send()

        for d in range(1, chips):
            to_mate(d, c).wait_send()
        for d in range(chips):
            to_pair(d, c).wait_send()
            to_pair(d, c).wait_recv()
        return carry

    lax.fori_loop(0, chunks, finish, 0)


def exchange(own, root, side, row_blocks, owners):
    depth, total = own.shape
    span = total // row_blocks
    chips = owners // 2
    flow = pltpu.VMEM((depth, total), jnp.float32)
    dma = pltpu.SemaphoreType.DMA
    line = [dma((CHUNKS,))] * 4
    memory = pl.BlockSpec(memory_space=pltpu.VMEM)
    scalars = pl.BlockSpec(memory_space=pltpu.SMEM)
    return pl.pallas_call(
        functools.partial(exchange_kernel, row_blocks, owners, CHUNKS),
        out_shape=(
            jax.ShapeDtypeStruct((depth, total), jnp.float32),
            jax.ShapeDtypeStruct((owners, depth, span), jnp.float32),
        ),
        in_specs=[scalars, scalars, memory],
        out_specs=(memory, memory),
        scratch_shapes=[flow] * 4 + line
        + [dma((chips - 1, CHUNKS))] * 2 + [dma((chips, CHUNKS))] * 2,
        compiler_params=pltpu.CompilerParams(
            collective_id=0, has_side_effects=True, vmem_limit_bytes=56 << 20
        ),
        cost_estimate=pl.CostEstimate(flops=0, bytes_accessed=400_000_000, transcendentals=0),
    )(root, side, own)


def product(a, b, dims):
    return lax.dot_general(a, b, (dims, ((), ())), precision=HIGHEST, preferred_element_type=jnp.float32)


def invert_tile(tile):
    size = tile.shape[0]
    row_of = lax.broadcasted_iota(jnp.int32, (size, size), 0)
    column_of = lax.broadcasted_iota(jnp.int32, (size, size), 1)
    right = jnp.where(row_of == column_of, 1.0, 0.0).astype(jnp.float32)
    sub = 8
    left_rows = [tile[i : i + sub] for i in range(0, size, sub)]
    right_rows = [right[i : i + sub] for i in range(0, size, sub)]
    index = lax.broadcasted_iota(jnp.int32, (sub, size), 0)
    scales = [jnp.zeros((sub, size), jnp.float32) for _ in left_rows]
    for k in range(size):
        at, inner = divmod(k, sub)
        pivot = jnp.broadcast_to(left_rows[at][inner : inner + 1, k : k + 1], (1, size))
        scale = 1.0 / pivot
        left_row = left_rows[at][inner : inner + 1, :] * scale
        right_row = right_rows[at][inner : inner + 1, :] * scale
        scales[at] = jnp.where(index == inner, lax.rsqrt(pivot), scales[at])
        for i in range(at, len(left_rows)):
            column = jnp.broadcast_to(left_rows[i][:, k : k + 1], (sub, size))
            if i == at:
                column = jnp.where(index > inner, column, 0.0)
            left_rows[i] = left_rows[i] - column * left_row
            right_rows[i] = right_rows[i] - column * right_row
    return jnp.concatenate([r * s for r, s in zip(right_rows, scales)], axis=0)


def factor_kernel(block_ref, inverse_ref, whole_ref, work, lower, tiles):
    size = block_ref.shape[0]
    count = size // TILE
    work[...] = block_ref[...]
    inverse_ref[...] = jnp.zeros_like(inverse_ref)

    def one(i, carry):
        at = pl.ds(pl.multiple_of(i * TILE, TILE), TILE)
        tile = invert_tile(work[at, at])
        tiles[i] = tile
        below = product(work[:, at], tile, ((1,), (1,)))
        row_of = lax.broadcasted_iota(jnp.int32, below.shape, 0)
        below = jnp.where(row_of >= (i + 1) * TILE, below, 0.0)
        lower[:, at] = below
        work[...] -= product(below, below, ((1,), (1,)))
        return carry

    lax.fori_loop(0, count, one, 0)
    for i in range(count):
        at = slice(i * TILE, (i + 1) * TILE)
        inverse_ref[at, at] = tiles[i]
        if i:
            done = slice(0, i * TILE)
            seen = product(lower[at, done], inverse_ref[done, done], ((1,), (0,)))
            inverse_ref[at, done] = -product(tiles[i], seen, ((1,), (0,)))
    inverse = inverse_ref[...]
    whole_ref[...] = product(inverse, inverse, ((0,), (0,)))


def factor(block):
    size = block.shape[0]
    square = jax.ShapeDtypeStruct((size, size), jnp.float32)
    return pl.pallas_call(
        factor_kernel,
        out_shape=(square, square),
        scratch_shapes=[
            pltpu.VMEM((size, size), jnp.float32),
            pltpu.VMEM((size, size), jnp.float32),
            pltpu.VMEM((size // TILE, TILE, TILE), jnp.float32),
        ],
        compiler_params=pltpu.CompilerParams(vmem_limit_bytes=32 << 20),
    )(block)


def update_kernel(keep_ref, old_ref, left_ref, right_ref, out_ref, right_parts):
    slots = keep_ref.shape[0]
    depth, rows = left_ref.shape
    width = right_ref.shape[1] // slots
    chunks = old_ref.shape[0] // rows
    halves = width // LANES

    @pl.when(pl.program_id(0) == 0)
    def _():
        for slot in range(slots):
            at = slice(slot * width, (slot + 1) * width)
            high, low = split(right_ref[:, at])
            right_parts[slot, :depth, :] = high
            right_parts[slot, depth : 2 * depth, :] = low
            right_parts[slot, 2 * depth :, :] = high

    high, low = split(left_ref[...].T)
    left_parts = jnp.concatenate([high, high, low], axis=1)
    for slot in range(slots):
        change = jnp.dot(left_parts, right_parts[slot], preferred_element_type=jnp.float32)
        keep = keep_ref[slot] > 0
        for half in range(halves):
            at = pl.ds(slot * halves + half, rows, stride=chunks)
            out_ref[at, :] = jnp.where(keep, old_ref[at, :], 0.0) - change[:, half * LANES : (half + 1) * LANES]


def update(flat, keep, left, right, width):
    groups, depth, span = left.shape
    slots = keep.shape[0]
    panels = groups * span // width
    lines = flat.shape[0] // panels
    return pl.pallas_call(
        update_kernel,
        out_shape=jax.ShapeDtypeStruct(flat.shape, jnp.float32),
        grid_spec=pltpu.PrefetchScalarGridSpec(
            num_scalar_prefetch=1,
            grid=(panels,),
            in_specs=[
                pl.BlockSpec((lines, LANES), lambda i, keep: (i, 0)),
                pl.BlockSpec((None, depth, width), lambda i, keep: (lax.rem(i, groups), 0, lax.div(i, groups))),
                pl.BlockSpec(right.shape, lambda i, keep: (0, 0)),
            ],
            out_specs=pl.BlockSpec((lines, LANES), lambda i, keep: (i, 0)),
            scratch_shapes=[pltpu.VMEM((slots, 3 * depth, width), jnp.bfloat16)],
        ),
        compiler_params=pltpu.CompilerParams(vmem_limit_bytes=56 << 20),
    )(keep, flat, left, right)


def local(covariance, panel_order):
    row_count, slots, _, width = covariance.shape
    owners = lax.axis_size("blk")
    row_blocks = lax.axis_size("rows")
    column_index = lax.axis_index("blk")
    row_index = lax.axis_index("rows")
    targets = [panel_order[section] for section in range(SECTIONS)]
    depth = SECTIONS * width
    row_panels = row_count // width
    roots = [target // row_panels for target in targets]

    strips = [
        lax.dynamic_slice_in_dim(covariance, (target % row_panels) * width, width, 0).reshape(width, slots * width)
        for target in targets
    ]
    own = jnp.concatenate(strips, axis=0)
    block = jnp.concatenate(
        [
            jnp.where(
                target % owners == column_index,
                lax.dynamic_slice_in_dim(own, (target // owners) * width, width, 1),
                0.0,
            )
            for target in targets
        ],
        axis=1,
    )
    here = jnp.repeat(jnp.stack(roots) == row_index, width)
    block = lax.psum(lax.psum(jnp.where(here[:, None], block, 0.0), "blk"), "rows")

    if row_panels % owners == 0 and owners % 2 == 0 and row_blocks > 1 and CHUNKS % SECTIONS == 0:
        share = CHUNKS // SECTIONS
        root = jnp.repeat(jnp.stack(roots) == row_index, share).astype(jnp.int32)
        side = jnp.repeat(jnp.stack(roots) < row_index, share).astype(jnp.int32)
        across, left = exchange(own, root, side, row_blocks, owners)
    else:
        across = lax.psum(jnp.where(here[:, None], own, 0.0), "rows")
        panels = jnp.concatenate(
            [
                jnp.where(
                    target % owners == column_index,
                    lax.dynamic_index_in_dim(covariance, target // owners, 1, keepdims=False)[:, 0],
                    0.0,
                )
                for target in targets
            ],
            axis=1,
        )
        left = lax.psum(panels, "blk").reshape(row_panels, width, depth).transpose(0, 2, 1)

    inverse, whole = factor(block)
    right = jnp.dot(whole, across, precision=HIGHEST).reshape(depth, slots, width)
    slot_panels = jnp.arange(slots, dtype=jnp.int32) * owners + column_index
    keep = jnp.ones((slots,), jnp.int32)
    for section, target in enumerate(targets):
        match = slot_panels == target
        keep = jnp.where(match, 0, keep)
        solved = -inverse[section * width : (section + 1) * width].T
        right = jnp.where(match[None, :, None], solved[:, None, :], right)
    flat = covariance.reshape(row_count * slots * (width // LANES), LANES)
    return update(flat, keep, left, right.reshape(depth, slots * width), width).reshape(covariance.shape)


def solution(mesh):
    return jax.shard_map(
        local,
        mesh=mesh,
        in_specs=(P("rows", None, "blk", None), P()),
        out_specs=P("rows", None, "blk", None),
        check_vma=False,
    )
```

```python
import functools

import jax
import jax.numpy as jnp
from jax import lax
from jax.experimental import pallas as pl
from jax.experimental.pallas import tpu as pltpu
from jax.sharding import PartitionSpec as P

SECTIONS = 2
LANES = 128
CHUNKS = 8
TILE = 128
MESH = pl.DeviceIdType.MESH
HIGHEST = lax.Precision.HIGHEST


def split(values):
    high = values.astype(jnp.bfloat16)
    low = (values - high.astype(jnp.float32)).astype(jnp.bfloat16)
    return high, low


def exchange_kernel(
    row_blocks, owners, chunks, root_ref, side_ref, own_ref, across_ref, left_ref,
    from_low, from_high, to_high, to_low, send_high, send_low, recv_low, recv_high,
    send_chip, recv_chip, send_pair, recv_pair,
):
    z = lax.axis_index("rows")
    me = lax.axis_index("blk")
    last = row_blocks - 1
    chips = owners // 2
    chip, core = me // 2, me % 2
    pair = chip * 2 + 1 - core
    rows = own_ref.shape[0] // chunks
    span = left_ref.shape[2]
    columns = pl.ds(pl.multiple_of(z * span, LANES), span)
    reach = jnp.maximum(z, last - z)

    def lines(c):
        return pl.ds(pl.multiple_of(c * rows, 8), rows)

    def mate(d):
        return (chip + d) % chips * 2 + core

    def source(d):
        return (chip + chips - d) % chips * 2 + core

    def along(src, dst, send, recv, c, step):
        return pltpu.make_async_remote_copy(
            src_ref=src.at[lines(c)], dst_ref=dst.at[lines(c)], send_sem=send.at[c], recv_sem=recv.at[c],
            device_id={"rows": z + step}, device_id_type=MESH,
        )

    def to_mate(d, c):
        return pltpu.make_async_remote_copy(
            src_ref=across_ref.at[lines(c), columns], dst_ref=left_ref.at[me, lines(c)],
            send_sem=send_chip.at[d - 1, c], recv_sem=recv_chip.at[d - 1, c],
            device_id={"blk": mate(d)}, device_id_type=MESH,
        )

    def to_pair(d, c):
        who = source(d)
        src = across_ref.at[lines(c), columns] if d == 0 else left_ref.at[who, lines(c)]
        return pltpu.make_async_remote_copy(
            src_ref=src, dst_ref=left_ref.at[who, lines(c)],
            send_sem=send_pair.at[d, c], recv_sem=recv_pair.at[d, c],
            device_id={"blk": pair}, device_id_type=MESH,
        )

    barrier = pltpu.get_barrier_semaphore()
    for d in range(1, chips):
        pl.semaphore_signal(barrier, inc=1, device_id={"blk": mate(d)}, device_id_type=MESH)
    pl.semaphore_signal(barrier, inc=1, device_id={"blk": pair}, device_id_type=MESH)

    @pl.when(z > 0)
    def _():
        pl.semaphore_signal(barrier, inc=1, device_id={"rows": z - 1}, device_id_type=MESH)

    @pl.when(z < last)
    def _():
        pl.semaphore_signal(barrier, inc=1, device_id={"rows": z + 1}, device_id_type=MESH)

    ends = jnp.where(z > 0, 1, 0) + jnp.where(z < last, 1, 0)
    pl.semaphore_wait(barrier, chips + ends)

    def valid(c):
        return jnp.logical_and(c >= 0, c < chunks)

    def step(t, carry):
        c = t - z

        @pl.when(valid(c))
        def _():
            @pl.when(z == 0)
            def _():
                along(own_ref, from_low, send_high, recv_low, c, 1).start()

            @pl.when(z > 0)
            def _():
                along(to_high, from_low, send_high, recv_low, c, 0).wait_recv()

            @pl.when(jnp.logical_and(z > 0, z < last))
            def _():
                here = root_ref[c] > 0
                to_high[lines(c), :] = jnp.where(here, own_ref[lines(c), :], from_low[lines(c), :])
                along(to_high, from_low, send_high, recv_low, c, 1).start()

        e = t - (last - z)

        @pl.when(valid(e))
        def _():
            @pl.when(z == last)
            def _():
                along(own_ref, from_high, send_low, recv_high, e, -1).start()

            @pl.when(z < last)
            def _():
                along(to_low, from_high, send_low, recv_high, e, 0).wait_recv()

            @pl.when(jnp.logical_and(z > 0, z < last))
            def _():
                here = root_ref[e] > 0
                to_low[lines(e), :] = jnp.where(here, own_ref[lines(e), :], from_high[lines(e), :])
                along(to_low, from_high, send_low, recv_high, e, -1).start()

        f = t - reach

        @pl.when(valid(f))
        def _():
            here = root_ref[f] > 0
            above = side_ref[f] > 0

            @pl.when(z == 0)
            def _():
                across_ref[lines(f), :] = jnp.where(here, own_ref[lines(f), :], from_high[lines(f), :])

            @pl.when(z == last)
            def _():
                across_ref[lines(f), :] = jnp.where(here, own_ref[lines(f), :], from_low[lines(f), :])

            @pl.when(jnp.logical_and(z > 0, z < last))
            def _():
                far = jnp.where(above, from_low[lines(f), :], from_high[lines(f), :])
                across_ref[lines(f), :] = jnp.where(here, own_ref[lines(f), :], far)

            left_ref[me, lines(f), :] = across_ref[lines(f), columns]
            for d in range(1, chips):
                to_mate(d, f).start()
            to_pair(0, f).start()

        g = f - 1

        @pl.when(valid(g))
        def _():
            for d in range(1, chips):
                to_mate(d, g).wait_recv()
                to_pair(d, g).start()

        return carry

    lax.fori_loop(0, chunks + last + 1, step, 0)

    def finish(c, carry):
        @pl.when(z < last)
        def _():
            along(own_ref, from_low, send_high, recv_low, c, 1).wait_send()

        @pl.when(z > 0)
        def _():
            along(own_ref, from_high, send_low, recv_high, c, -1).wait_send()

        for d in range(1, chips):
            to_mate(d, c).wait_send()
        for d in range(chips):
            to_pair(d, c).wait_send()
            to_pair(d, c).wait_recv()
        return carry

    lax.fori_loop(0, chunks, finish, 0)


def exchange(own, root, side, row_blocks, owners):
    depth, total = own.shape
    span = total // row_blocks
    chips = owners // 2
    flow = pltpu.VMEM((depth, total), jnp.float32)
    dma = pltpu.SemaphoreType.DMA
    line = [dma((CHUNKS,))] * 4
    memory = pl.BlockSpec(memory_space=pltpu.VMEM)
    scalars = pl.BlockSpec(memory_space=pltpu.SMEM)
    return pl.pallas_call(
        functools.partial(exchange_kernel, row_blocks, owners, CHUNKS),
        out_shape=(
            jax.ShapeDtypeStruct((depth, total), jnp.float32),
            jax.ShapeDtypeStruct((owners, depth, span), jnp.float32),
        ),
        in_specs=[scalars, scalars, memory],
        out_specs=(memory, memory),
        scratch_shapes=[flow] * 4 + line
        + [dma((chips - 1, CHUNKS))] * 2 + [dma((chips, CHUNKS))] * 2,
        compiler_params=pltpu.CompilerParams(
            collective_id=0, has_side_effects=True, vmem_limit_bytes=56 << 20
        ),
        cost_estimate=pl.CostEstimate(flops=0, bytes_accessed=400_000_000, transcendentals=0),
    )(root, side, own)


def product(a, b, dims):
    return lax.dot_general(a, b, (dims, ((), ())), precision=HIGHEST, preferred_element_type=jnp.float32)


def invert_tile(tile):
    size = tile.shape[0]
    row_of = lax.broadcasted_iota(jnp.int32, (size, size), 0)
    column_of = lax.broadcasted_iota(jnp.int32, (size, size), 1)
    right = jnp.where(row_of == column_of, 1.0, 0.0).astype(jnp.float32)
    sub = 8
    left_rows = [tile[i : i + sub] for i in range(0, size, sub)]
    right_rows = [right[i : i + sub] for i in range(0, size, sub)]
    index = lax.broadcasted_iota(jnp.int32, (sub, size), 0)
    scales = [jnp.zeros((sub, size), jnp.float32) for _ in left_rows]
    for k in range(size):
        at, inner = divmod(k, sub)
        pivot = jnp.broadcast_to(left_rows[at][inner : inner + 1, k : k + 1], (1, size))
        scale = 1.0 / pivot
        left_row = left_rows[at][inner : inner + 1, :] * scale
        right_row = right_rows[at][inner : inner + 1, :] * scale
        scales[at] = jnp.where(index == inner, lax.rsqrt(pivot), scales[at])
        for i in range(at, len(left_rows)):
            column = jnp.broadcast_to(left_rows[i][:, k : k + 1], (sub, size))
            if i == at:
                column = jnp.where(index > inner, column, 0.0)
            left_rows[i] = left_rows[i] - column * left_row
            right_rows[i] = right_rows[i] - column * right_row
    return jnp.concatenate([r * s for r, s in zip(right_rows, scales)], axis=0)


def factor_kernel(block_ref, inverse_ref, whole_ref, work, lower, tiles):
    size = block_ref.shape[0]
    count = size // TILE
    work[...] = block_ref[...]
    inverse_ref[...] = jnp.zeros_like(inverse_ref)

    def one(i, carry):
        at = pl.ds(pl.multiple_of(i * TILE, TILE), TILE)
        tile = invert_tile(work[at, at])
        tiles[i] = tile
        below = product(work[:, at], tile, ((1,), (1,)))
        row_of = lax.broadcasted_iota(jnp.int32, below.shape, 0)
        below = jnp.where(row_of >= (i + 1) * TILE, below, 0.0)
        lower[:, at] = below
        work[...] -= product(below, below, ((1,), (1,)))
        return carry

    lax.fori_loop(0, count, one, 0)
    for i in range(count):
        at = slice(i * TILE, (i + 1) * TILE)
        inverse_ref[at, at] = tiles[i]
        if i:
            done = slice(0, i * TILE)
            seen = product(lower[at, done], inverse_ref[done, done], ((1,), (0,)))
            inverse_ref[at, done] = -product(tiles[i], seen, ((1,), (0,)))
    inverse = inverse_ref[...]
    whole_ref[...] = product(inverse, inverse, ((0,), (0,)))


def factor(block):
    size = block.shape[0]
    square = jax.ShapeDtypeStruct((size, size), jnp.float32)
    return pl.pallas_call(
        factor_kernel,
        out_shape=(square, square),
        scratch_shapes=[
            pltpu.VMEM((size, size), jnp.float32),
            pltpu.VMEM((size, size), jnp.float32),
            pltpu.VMEM((size // TILE, TILE, TILE), jnp.float32),
        ],
        compiler_params=pltpu.CompilerParams(vmem_limit_bytes=32 << 20),
    )(block)


def update_kernel(keep_ref, old_ref, left_ref, right_ref, out_ref, right_parts):
    slots = keep_ref.shape[0]
    depth, rows = left_ref.shape
    width = right_ref.shape[1] // slots
    chunks = old_ref.shape[0] // rows
    halves = width // LANES

    @pl.when(pl.program_id(0) == 0)
    def _():
        for slot in range(slots):
            at = slice(slot * width, (slot + 1) * width)
            high, low = split(right_ref[:, at])
            right_parts[slot, :depth, :] = high
            right_parts[slot, depth : 2 * depth, :] = low
            right_parts[slot, 2 * depth :, :] = high

    high, low = split(left_ref[...].T)
    left_parts = jnp.concatenate([high, high, low], axis=1)
    for slot in range(slots):
        change = jnp.dot(left_parts, right_parts[slot], preferred_element_type=jnp.float32)
        keep = keep_ref[slot] > 0
        for half in range(halves):
            at = pl.ds(slot * halves + half, rows, stride=chunks)
            out_ref[at, :] = jnp.where(keep, old_ref[at, :], 0.0) - change[:, half * LANES : (half + 1) * LANES]


def update(flat, keep, left, right, width):
    groups, depth, span = left.shape
    slots = keep.shape[0]
    panels = groups * span // width
    lines = flat.shape[0] // panels
    return pl.pallas_call(
        update_kernel,
        out_shape=jax.ShapeDtypeStruct(flat.shape, jnp.float32),
        grid_spec=pltpu.PrefetchScalarGridSpec(
            num_scalar_prefetch=1,
            grid=(panels,),
            in_specs=[
                pl.BlockSpec((lines, LANES), lambda i, keep: (i, 0)),
                pl.BlockSpec((None, depth, width), lambda i, keep: (lax.rem(i, groups), 0, lax.div(i, groups))),
                pl.BlockSpec(right.shape, lambda i, keep: (0, 0)),
            ],
            out_specs=pl.BlockSpec((lines, LANES), lambda i, keep: (i, 0)),
            scratch_shapes=[pltpu.VMEM((slots, 3 * depth, width), jnp.bfloat16)],
        ),
        compiler_params=pltpu.CompilerParams(vmem_limit_bytes=56 << 20),
    )(keep, flat, left, right)


def local(covariance, panel_order):
    row_count, slots, _, width = covariance.shape
    owners = lax.axis_size("blk")
    row_blocks = lax.axis_size("rows")
    column_index = lax.axis_index("blk")
    row_index = lax.axis_index("rows")
    targets = [panel_order[section] for section in range(SECTIONS)]
    depth = SECTIONS * width
    row_panels = row_count // width
    roots = [target // row_panels for target in targets]

    strips = [
        lax.dynamic_slice_in_dim(covariance, (target % row_panels) * width, width, 0).reshape(width, slots * width)
        for target in targets
    ]
    own = jnp.concatenate(strips, axis=0)
    block = jnp.concatenate(
        [
            jnp.where(
                target % owners == column_index,
                lax.dynamic_slice_in_dim(own, (target // owners) * width, width, 1),
                0.0,
            )
            for target in targets
        ],
        axis=1,
    )
    here = jnp.repeat(jnp.stack(roots) == row_index, width)
    block = lax.psum(jnp.where(here[:, None], block, 0.0), ("blk", "rows"))

    if row_panels % owners == 0 and owners % 2 == 0 and row_blocks > 1 and CHUNKS % SECTIONS == 0:
        share = CHUNKS // SECTIONS
        root = jnp.repeat(jnp.stack(roots) == row_index, share).astype(jnp.int32)
        side = jnp.repeat(jnp.stack(roots) < row_index, share).astype(jnp.int32)
        across, left = exchange(own, root, side, row_blocks, owners)
    else:
        across = lax.psum(jnp.where(here[:, None], own, 0.0), "rows")
        panels = jnp.concatenate(
            [
                jnp.where(
                    target % owners == column_index,
                    lax.dynamic_index_in_dim(covariance, target // owners, 1, keepdims=False)[:, 0],
                    0.0,
                )
                for target in targets
            ],
            axis=1,
        )
        left = lax.psum(panels, "blk").reshape(row_panels, width, depth).transpose(0, 2, 1)

    inverse, whole = factor(block)
    right = jnp.dot(whole, across, precision=HIGHEST).reshape(depth, slots, width)
    slot_panels = jnp.arange(slots, dtype=jnp.int32) * owners + column_index
    keep = jnp.ones((slots,), jnp.int32)
    for section, target in enumerate(targets):
        match = slot_panels == target
        keep = jnp.where(match, 0, keep)
        solved = -inverse[section * width : (section + 1) * width].T
        right = jnp.where(match[None, :, None], solved[:, None, :], right)
    flat = covariance.reshape(row_count * slots * (width // LANES), LANES)
    return update(flat, keep, left, right.reshape(depth, slots * width), width).reshape(covariance.shape)


def solution(mesh):
    return jax.shard_map(
        local,
        mesh=mesh,
        in_specs=(P("rows", None, "blk", None), P()),
        out_specs=P("rows", None, "blk", None),
        check_vma=False,
    )
```
